32 devices in a mesh: groups: 2 (over y), batch: 16 (over z, x, core).
Axes of the slice: x: 2, y: 2, z: 4, core: 2. Of those that a mesh axis runs over, the one named last changes fastest.
Arguments:
- queries: bfloat16 [64, 34, 8192], P(('groups', 'batch')), parts along dimension 0, may hold values from -6 to 6
- key_vectors: bfloat16 [64, 34, 8192], P(('groups', 'batch')), parts along dimension 0, may hold values from -0.5 to 0.5
- values: bfloat16 [64, 34, 8192], P(('groups', 'batch')), parts along dimension 0, may hold values from -6 to 6
- gate_logits: bfloat16 [64, 34, 8192], P(('groups', 'batch')), parts along dimension 0, may hold values from -6 to 6
- decay_rates: float32 [64], replicated, may hold values from 0.003 to 0.08
- norm_gain: float32 [8192], replicated, may hold values from 0.1 to 1.9
- pool_states: bfloat16 [32, 8192, 128], P(('groups', 'batch')), parts along dimension 0, may hold values from -1.75 to 1.75
- pool_entry: int32 [64], P(('groups', 'batch')), parts along dimension 0, may hold values from 0 to 15
Outputs:
- mixed: bfloat16 [64, 34, 8192], P(('groups', 'batch')), parts along dimension 0
- new_states: bfloat16 [64, 8192, 128], P('groups', 'batch'), parts along dimension 0
The draws below stay inside these ranges and needn't reach their ends.
There are 2 independent parts, one for each index of `groups`. The reference program is written for one: setup_inputs(seed, part) draws one part's arguments, and reference() takes and returns one part's arrays. A program takes and returns all parts, laid end to end along the dimension named above; an argument that names none is the same for every part. Nothing has to cross between parts.
Inputs may be any that keep to these rules, and one draw needn't show every extreme that they name: `pool_entry`: entry e is the only entry of the pool shard on batch device e; several requests may name the same entry.
All inputs are finite; a program needn't handle non-finite values.
Results may differ from the reference program's by a relative error of at most 0.001.
Values may be sent and summed in bfloat16 or wider, within the bound.
No kernel may reach another device: no remote copies, remote signals or barrier semaphores. Data moves between devices by JAX's collectives and lax.ppermute only.
A program may use at most 64 MiB of HBM per device.

```python
import math
import jax
import jax.numpy as jnp
import numpy as np
from jax import lax

HEADS = 64
HEAD = 128
REQS = 32
ENTRIES = 16
LEN = 34
WIDTH = 8192


def place_ends(values, own_key, least, largest):
    dims = values.shape
    place = [jax.random.randint(jax.random.fold_in(own_key, axis), (), 0, dims[axis]) for axis in range(len(dims))]
    values = values.at[tuple(place)].set(least)
    longest = dims.index(max(dims))
    place[longest] = (place[longest] + 1) % dims[longest]
    return values.at[tuple(place)].set(largest)


def block_scale(rng, dims, split, low, top_value):
    gain = 1.0
    for axis_at, blocks in split:
        heights = jax.random.uniform(jax.random.fold_in(jax.random.fold_in(rng, 6), axis_at), (blocks,), jnp.float32, low / len(split), top_value / len(split))
        gain = gain * jnp.repeat(jnp.exp(heights), dims[axis_at] // blocks).reshape((-1,) + (1,) * (len(dims) - 1 - axis_at))
    return gain


def cumulative_ranks(count, lean):
    weights = [(1 << 20) // math.isqrt(rank ** lean) + 1 for rank in range(1, count + 1)]
    width = 1 + sum(weights) // (1 << 30)
    return np.cumsum(np.array([max(1, weight // width) for weight in weights]))


def skewed_ids(stream_key, shape, amount, lean):
    listing = cumulative_ranks(amount, lean)
    lot = jax.random.randint(jax.random.fold_in(stream_key, 1), shape, 0, int(listing[amount - 1]))
    standing = jnp.searchsorted(jnp.asarray(listing, jnp.int32), lot, side="right")
    return jax.random.permutation(jax.random.fold_in(stream_key, 2), amount)[standing].astype(jnp.int32)


def normal_values(own_key, shape, scale, limit, pieces=(), kind=jnp.bfloat16):
    gain = block_scale(own_key, shape, pieces, -0.22, 0.18) if pieces else 1.0
    values = jax.random.normal(own_key, shape, jnp.float32) * scale * gain
    return jnp.minimum(jnp.maximum(values, -limit), limit).astype(kind)


def setup_inputs(seed: int = 0, part: int = 0) -> dict:
    key_of = jax.random.split(jax.random.key(seed), 9)
    part_splits = jax.random.split(jax.random.fold_in(key_of[8], part), 9)
    queries = normal_values(part_splits[0], (REQS, LEN, WIDTH), 1.0, 6.0, ((0, 16),))
    key_vectors = normal_values(part_splits[1], (REQS, LEN, WIDTH), (HEAD ** -0.5), 0.5, ((0, 16),))
    values = normal_values(part_splits[2], (REQS, LEN, WIDTH), 1.0, 6.0, ((0, 16),))
    gate_logits = normal_values(part_splits[3], (REQS, LEN, WIDTH), 1.0, 6.0, ((0, 16),))
    decay_rates = jnp.clip(jnp.exp(jax.random.uniform(key_of[4], (HEADS,), jnp.float32, math.log(0.003), math.log(0.08))), 0.003, 0.08)
    norm_gain = jnp.clip(1.0 + 0.18 * jax.random.normal(key_of[5], (WIDTH,), jnp.float32), 0.1, 1.9)
    pool_states = normal_values(part_splits[6], (ENTRIES, WIDTH, HEAD), 0.3, 1.75, ((0, 16),))
    pool_entry = place_ends(skewed_ids(part_splits[7], (REQS,), ENTRIES, 2), jax.random.fold_in(part_splits[7], 3), 0, ENTRIES - 1).astype(jnp.int32)
    return dict(queries=queries, key_vectors=key_vectors, values=values, gate_logits=gate_logits, decay_rates=decay_rates, norm_gain=norm_gain, pool_states=pool_states, pool_entry=pool_entry)


def finish_output(attended, gate_logits, norm_gain):
    mean_square = lax.optimization_barrier(jnp.mean(attended * attended, axis=-1, keepdims=True))
    scaled = attended * lax.rsqrt(mean_square + 1e-05) * norm_gain
    return (scaled * jax.nn.sigmoid(gate_logits.astype(jnp.float32))).astype(jnp.bfloat16)

def reference(queries, key_vectors, values, gate_logits, decay_rates, norm_gain, pool_states, pool_entry):
    head_count = decay_rates.shape[0]
    length = queries.shape[1]
    head_size = pool_states.shape[2]
    highest = lax.Precision.HIGHEST

    def one_request(items):
        query_rows, key_rows, value_rows, gate_rows, entry_id = items
        resumed = lax.dynamic_index_in_dim(pool_states, entry_id.astype(jnp.int32), 0, keepdims=False)
        resumed = resumed.astype(jnp.float32).reshape(head_count, head_size, head_size)
        query_heads = query_rows.astype(jnp.float32).reshape(length, head_count, head_size)
        key_heads = key_rows.astype(jnp.float32).reshape(length, head_count, head_size)
        value_heads = value_rows.astype(jnp.float32).reshape(length, head_count, head_size)
        positions = jnp.arange(1, length + 1).astype(jnp.float32)
        decay_now = jnp.exp(-positions[:, None] * decay_rates[None, :])
        from_state = jnp.einsum('thd,hde->the', query_heads, resumed, precision=highest) * decay_now[:, :, None]
        distance = positions[:, None] - positions[None, :]
        decay_pair = jnp.where((distance >= 0.0)[:, :, None], jnp.exp(-jnp.maximum(distance, 0.0)[:, :, None] * decay_rates), 0.0)
        scores = jnp.einsum('thd,shd->tsh', query_heads, key_heads, precision=highest) * decay_pair
        in_block = jnp.einsum('tsh,she->the', scores, value_heads, precision=highest)
        attended = (from_state + in_block).reshape(length, head_count * head_size)
        tail_decay = jnp.exp(-(float(length) - positions)[:, None] * decay_rates[None, :])
        weighted_keys = key_heads * tail_decay[:, :, None]
        updated = jnp.exp(-float(length) * decay_rates)[:, None, None] * resumed
        updated = updated + jnp.einsum('shd,she->hde', weighted_keys, value_heads, precision=highest)
        mixed_rows = finish_output(attended, gate_rows, norm_gain)
        return (mixed_rows, updated.reshape(head_count * head_size, head_size).astype(jnp.bfloat16))
    mixed, new_states = lax.map(one_request, (queries, key_vectors, values, gate_logits, pool_entry))
    return (mixed, new_states)
```

```python
import functools

import jax
import jax.numpy as jnp
from jax import lax
from jax.experimental import pallas as pl
from jax.experimental.pallas import tpu as pltpu
from jax.sharding import PartitionSpec as P


ANY = pl.BlockSpec(memory_space=pl.ANY)
SMEM = pl.BlockSpec(memory_space=pltpu.SMEM)
VMEM = pl.BlockSpec(memory_space=pltpu.VMEM)
F32 = jnp.float32
BF16 = jnp.bfloat16
NT = (((1,), (1,)), ((), ()))
TN = (((0,), (0,)), ((), ()))


def finish_output(attended, gate_logits, norm_gain):
    mean_square = jnp.mean(attended * attended, axis=-1, keepdims=True)
    scaled = attended * lax.rsqrt(mean_square + 1e-05) * norm_gain
    return (scaled * jax.nn.sigmoid(gate_logits.astype(jnp.float32))).astype(jnp.bfloat16)


def attend(query_part, key_part, value_part, resumed, rates_here):
    length = query_part.shape[1]
    highest = lax.Precision.HIGHEST
    positions = jnp.arange(1, length + 1).astype(jnp.float32)
    decay_now = jnp.exp(-positions[:, None] * rates_here[None, :])
    from_state = jnp.einsum(
        "rtgd,rgde->rtge", query_part, resumed, preferred_element_type=jnp.float32
    )
    from_state = from_state * decay_now[None, :, :, None]
    key_wide = key_part.astype(jnp.float32)
    value_wide = value_part.astype(jnp.float32)
    distance = positions[:, None] - positions[None, :]
    decay_pair = jnp.where(
        (distance >= 0.0)[:, :, None],
        jnp.exp(-jnp.maximum(distance, 0.0)[:, :, None] * rates_here),
        0.0,
    )
    scores = (
        jnp.einsum("rtgd,rsgd->rtsg", query_part, key_part, preferred_element_type=jnp.float32)
        * decay_pair[None]
    )
    in_block = jnp.einsum("rtsg,rsge->rtge", scores, value_wide, precision=highest)
    tail_decay = jnp.exp(-(float(length) - positions)[:, None] * rates_here[None, :])
    weighted_keys = key_wide * tail_decay[None, :, :, None]
    updated = jnp.exp(-float(length) * rates_here)[None, :, None, None] * resumed.astype(
        jnp.float32
    )
    updated = updated + jnp.einsum("rsgd,rsge->rgde", weighted_keys, value_wide, precision=highest)
    return (from_state + in_block, updated)


def general(
    queries, key_vectors, values, gate_logits, decay_rates, norm_gain, pool_states, pool_entry
):
    req_dev, length, feature_width = queries.shape
    head_count = decay_rates.shape[0]
    head_size = pool_states.shape[2]
    entries = lax.all_gather(pool_entry, "batch", axis=0, tiled=True)
    spread = lax.all_to_all(pool_states, "batch", split_axis=1, concat_axis=0, tiled=True)
    chosen = jnp.take(spread, entries, axis=0)
    resumed = lax.all_to_all(chosen, "batch", split_axis=0, concat_axis=1, tiled=True)
    resumed = resumed.reshape(req_dev, head_count, head_size, head_size)
    shaped = (req_dev, length, head_count, head_size)
    attended, updated = attend(
        queries.reshape(shaped),
        key_vectors.reshape(shaped),
        values.reshape(shaped),
        resumed,
        decay_rates,
    )
    attended = attended.reshape(req_dev, length, feature_width)
    local_states = updated.astype(jnp.bfloat16).reshape(req_dev, feature_width, head_size)
    new_states = lax.all_to_all(local_states, "batch", split_axis=1, concat_axis=0, tiled=True)
    mixed = finish_output(attended, gate_logits, norm_gain)
    return (mixed, new_states)


def call(kernel, outs, in_specs, out_specs, scratch, args, flops=0, moved=0, aliases=None):
    return pl.pallas_call(
        kernel,
        out_shape=outs,
        in_specs=in_specs,
        out_specs=out_specs,
        scratch_shapes=scratch,
        input_output_aliases=aliases or {},
        compiler_params=pltpu.CompilerParams(vmem_limit_bytes=48 * 1024 * 1024),
        cost_estimate=pl.CostEstimate(flops=flops, bytes_accessed=moved, transcendentals=0),
    )(*args)


def row_rates(rates, group, heads):
    head = lax.broadcasted_iota(jnp.int32, (8, 128), 0) // (8 // heads)
    rate = jnp.full((8, 128), rates[group * heads], F32)
    for h in range(1, heads):
        rate = jnp.where(head == h, rates[group * heads + h], rate)
    return rate


def pack_start(place, pool, queries, n):
    half = n // 2
    _, rows, lanes = pool.shape
    length = queries.shape[0]

    def kernel(place, pool, queries, *refs):
        pool_out, query_out = refs[:half], refs[half : 2 * half]
        pool_buf, query_buf, load, store, query_store = refs[2 * half :]
        spot = lax.rem(place[0], half)
        loads = [
            pltpu.make_async_copy(pool.at[pl.ds(w * half, half)], pool_buf.at[pl.ds(w * half, half)], load.at[w])
            for w in range(2)
        ]
        loads.append(pltpu.make_async_copy(queries, query_buf, load.at[2]))
        for copy in loads:
            copy.start()
        stores = []
        for w in range(2):
            loads[w].wait()
            for k in range(half):
                there = lax.rem(spot + k, half) + w * half
                stores.append(pltpu.make_async_copy(pool_buf.at[there], pool_out[k].at[w], store.at[k, w]))
                stores[-1].start()
        loads[2].wait()
        for w in range(2):
            for k in range(half):
                there = lax.rem(spot + k, half) + w * half
                stores.append(
                    pltpu.make_async_copy(query_buf.at[:, there], query_out[k].at[w], query_store.at[k, w])
                )
                stores[-1].start()
        for copy in stores:
            copy.wait()

    outs = [jax.ShapeDtypeStruct((2, rows, lanes), BF16)] * half
    outs += [jax.ShapeDtypeStruct((2, length, 8, lanes), BF16)] * half
    scratch = [
        pltpu.VMEM(pool.shape, BF16),
        pltpu.VMEM(queries.shape, BF16),
        pltpu.SemaphoreType.DMA((3,)),
        pltpu.SemaphoreType.DMA((half, 2)),
        pltpu.SemaphoreType.DMA((half, 2)),
    ]
    got = call(
        kernel, outs, [SMEM, ANY, ANY], [ANY] * (2 * half), scratch, (place, pool, queries),
        moved=4 * pool.size + 4 * queries.size,
    )
    return got[:half], got[half:]


def pack_pairs(place, keys, values, after, n):
    length, _, _, lanes = keys.shape

    def kernel(place, keys, values, *refs):
        outs = refs[len(after) : len(after) + n]
        buf, load, store = refs[len(after) + n :]
        me = place[0]
        loads = [
            pltpu.make_async_copy(source, buf.at[w], load.at[w]) for w, source in enumerate((keys, values))
        ]
        for copy in loads:
            copy.start()
        stores = []
        for w in range(2):
            loads[w].wait()
            for k in range(n):
                there = lax.rem(me + k, n)
                stores.append(pltpu.make_async_copy(buf.at[w, :, there], outs[k].at[w], store.at[k, w]))
                stores[-1].start()
        for copy in stores:
            copy.wait()

    outs = [jax.ShapeDtypeStruct((2, length, 8, lanes), BF16)] * n
    scratch = [
        pltpu.VMEM((2,) + keys.shape, BF16),
        pltpu.SemaphoreType.DMA((2,)),
        pltpu.SemaphoreType.DMA((n, 2)),
    ]
    return call(
        kernel, outs, [SMEM] + [ANY] * (2 + len(after)), [ANY] * n, scratch, (place, keys, values, *after),
        moved=8 * keys.size,
    )


def in_block(rates, queries, keys, values, after, heads):
    length, groups, _, lanes = queries.shape
    rows = length * 8

    def kernel(rates, q_ref, k_ref, v_ref, after_ref, out_ref, gap):
        group = pl.program_id(0)

        @pl.when(group == 0)
        def _():
            row = lax.broadcasted_iota(jnp.int32, (rows, rows), 0)
            column = lax.broadcasted_iota(jnp.int32, (rows, rows), 1)
            distance = (row >> 3) - (column >> 3)
            seen = ((row & 7) == (column & 7)) & (distance >= 0)
            gap[...] = jnp.where(seen, distance, -1).astype(F32)

        def flat(ref):
            return ref[:, 0].astype(F32).reshape(rows, lanes).astype(BF16)

        q, k, v = flat(q_ref), flat(k_ref), flat(v_ref)
        rate = row_rates(rates, group, heads)[:, :1]
        rate = jnp.broadcast_to(rate[None], (length, 8, 1)).reshape(rows, 1)
        distance = gap[...]
        decay = jnp.where(distance >= 0.0, jnp.exp(-jnp.maximum(distance, 0.0) * rate), 0.0)
        scores = lax.dot_general(q, k, NT, preferred_element_type=F32) * decay
        coarse = scores.astype(BF16)
        fine = (scores - coarse.astype(F32)).astype(BF16)
        total = jnp.dot(coarse, v, preferred_element_type=F32)
        total = total + jnp.dot(fine, v, preferred_element_type=F32)
        out_ref[0] = total.reshape(length, 8, lanes)

    block = pl.BlockSpec((length, 1, 8, lanes), lambda g: (0, g, 0, 0))
    return pl.pallas_call(
        kernel,
        grid=(groups,),
        out_shape=jax.ShapeDtypeStruct((groups, length, 8, lanes), F32),
        in_specs=[SMEM, block, block, block, ANY],
        out_specs=pl.BlockSpec((1, length, 8, lanes), lambda g: (g, 0, 0, 0)),
        scratch_shapes=[pltpu.VMEM((rows, rows), F32)],
        compiler_params=pltpu.CompilerParams(vmem_limit_bytes=32 * 1024 * 1024),
        cost_estimate=pl.CostEstimate(
            flops=6 * groups * rows * rows * lanes, bytes_accessed=10 * queries.size, transcendentals=0
        ),
    )(rates, queries, keys, values, after)


def from_state(place, entries, rates, pools, queries, n, heads):
    half = n // 2
    width = pools[0].shape[1]
    _, length, _, lanes = queries[0].shape
    rows = length * 8
    reqs = 8 // heads

    def kernel(place, entries, rates, *refs):
        pool_in, query_in, outs = refs[:n], refs[n : n + half], refs[n + half : n + 2 * half]
        pool_buf, query_buf, out_buf, pool_sem, query_sem, out_sem = refs[n + 2 * half :]
        me = place[0]
        spot = lax.rem(me, half)
        loads = [pltpu.make_async_copy(pool_in[k], pool_buf.at[k], pool_sem.at[k]) for k in range(n)]
        loads += [pltpu.make_async_copy(query_in[k], query_buf.at[k], query_sem.at[k]) for k in range(half)]
        for copy in loads:
            copy.start()
        for copy in loads:
            copy.wait()
        row = lax.broadcasted_iota(jnp.int32, (length, 8, lanes), 1)
        time = (lax.broadcasted_iota(jnp.int32, (length, 8, lanes), 0) + 1).astype(F32)

        for w in range(2):
            decay = jnp.exp(-time * row_rates(rates, spot + w * half, heads)[None])

            def step(k, carry):
                source = lax.rem(spot - k + half, half) + (me - spot)
                slots = [lax.rem(me - entries[source * reqs + i] + n, n) for i in range(reqs)]
                q = query_buf[k, w].astype(F32)
                total = jnp.zeros((rows, lanes), F32)
                for h in range(heads):
                    parts, states = [], []
                    for i in range(reqs):
                        parts.append(jnp.where(row == h * reqs + i, q, 0.0).reshape(rows, lanes).astype(BF16))
                        states.append(pool_buf[slots[i], w, h * lanes : (h + 1) * lanes, :])
                    total = total + jnp.dot(
                        jnp.concatenate(parts, axis=1),
                        jnp.concatenate(states, axis=0),
                        preferred_element_type=F32,
                    )
                out_buf[k, w] = total.reshape(length, 8, lanes) * decay
                return carry

            lax.fori_loop(0, half, step, 0)
        stores = [pltpu.make_async_copy(out_buf.at[k], outs[k], out_sem.at[k]) for k in range(half)]
        for copy in stores:
            copy.start()
        for copy in stores:
            copy.wait()

    outs = [jax.ShapeDtypeStruct((2, length, 8, lanes), F32)] * half
    scratch = [
        pltpu.VMEM((n, 2, width, lanes), BF16),
        pltpu.VMEM((half, 2, length, 8, lanes), BF16),
        pltpu.VMEM((half, 2, length, 8, lanes), F32),
        pltpu.SemaphoreType.DMA((n,)),
        pltpu.SemaphoreType.DMA((half,)),
        pltpu.SemaphoreType.DMA((half,)),
    ]
    return call(
        kernel, outs, [SMEM] * 3 + [ANY] * (n + half), [ANY] * half, scratch,
        (place, entries, rates, *pools, *queries),
        flops=4 * n * rows * lanes * 8 * lanes, moved=4 * n * width * lanes,
    )


def next_states(place, entries, rates, pools, pairs, kept, ks, n, heads):
    width = pools[0].shape[1]
    _, length, _, lanes = pairs[0].shape
    rows = length * 8
    reqs = 8 // heads
    count = len(ks)
    half = n // 2
    extra = 0 if kept is None else 1

    def kernel(place, entries, rates, *refs):
        pool_in, pair_in = refs[:n], refs[n : n + count]
        out = refs[n + count + extra]
        pool_buf, pair_buf, key_buf, value_buf, out_buf, pool_sem, pair_sem, out_sem = refs[n + count + extra + 1 :]
        me = place[0]
        own = me // half
        loads = [pltpu.make_async_copy(pool_in[k].at[own], pool_buf.at[k], pool_sem.at[k]) for k in range(n)]
        loads += [pltpu.make_async_copy(pair_in[k], pair_buf.at[k], pair_sem.at[k]) for k in range(count)]
        for copy in loads:
            copy.start()
        for copy in loads:
            copy.wait()
        left = (length - 1 - lax.broadcasted_iota(jnp.int32, (length, 8, lanes), 0)).astype(F32)
        weight = jnp.exp(-left * row_rates(rates, me, heads)[None])

        def step(c, carry):
            source = lax.rem(me - (ks[0] + c) + n, n)
            key_buf[...] = (pair_buf[c, 0].astype(F32) * weight).reshape(rows, lanes)
            value_buf[...] = pair_buf[c, 1].astype(F32).reshape(rows, lanes)
            for i in range(reqs):
                slot = lax.rem(me - entries[source * reqs + i] + n, n)
                for h in range(heads):
                    r = h * reqs + i
                    key = key_buf[pl.ds(r, length, stride=8), :]
                    value = value_buf[pl.ds(r, length, stride=8), :].astype(BF16)
                    coarse = key.astype(BF16)
                    fine = (key - coarse.astype(F32)).astype(BF16)
                    both = lax.dot_general(
                        jnp.concatenate([coarse, fine], axis=1), value, TN, preferred_element_type=F32
                    )
                    shrink = jnp.exp(jnp.full((1, lanes), -float(length) * rates[me * heads + h], F32))
                    start = pool_buf[slot, h * lanes : (h + 1) * lanes, :].astype(F32)
                    state = shrink * start + (both[:lanes] + both[lanes:])
                    out_buf[c * reqs + i, h * lanes : (h + 1) * lanes, :] = state.astype(BF16)
                pltpu.make_async_copy(
                    out_buf.at[c * reqs + i], out.at[source * reqs + i], out_sem.at[c * reqs + i]
                ).start()
            return carry

        lax.fori_loop(0, count, step, 0)
        for c in range(count * reqs):
            pltpu.make_async_copy(out_buf.at[c], out.at[c], out_sem.at[c]).wait()

    scratch = [
        pltpu.VMEM((n, width, lanes), BF16),
        pltpu.VMEM((count, 2, length, 8, lanes), BF16),
        pltpu.VMEM((rows, lanes), F32),
        pltpu.VMEM((rows, lanes), F32),
        pltpu.VMEM((count * reqs, width, lanes), BF16),
        pltpu.SemaphoreType.DMA((n,)),
        pltpu.SemaphoreType.DMA((count,)),
        pltpu.SemaphoreType.DMA((count * reqs,)),
    ]
    args = (place, entries, rates, *pools, *pairs)
    aliases = None
    if kept is not None:
        aliases = {len(args): 0}
        args += (kept,)
    return call(
        kernel, jax.ShapeDtypeStruct((n * reqs, width, lanes), BF16),
        [SMEM] * 3 + [ANY] * (len(args) - 3), ANY, scratch, args,
        flops=count * 8 * 4 * lanes * lanes * length, moved=2 * n * width * lanes + 4 * count * width * lanes,
        aliases=aliases,
    )


def finish(place, products, local, gates, gain, n, heads):
    half = n // 2
    groups, length, _, lanes = local.shape
    reqs = 8 // heads
    width = groups * heads * lanes

    def kernel(place, *refs):
        products, local, gates, gain, out, total = refs[:half], *refs[half:]
        spot = lax.rem(place[0], half)
        square = jnp.zeros((length, 8, lanes), F32)
        for k in range(half):
            for w in range(2):
                group = lax.rem(spot + k, half) + w * half
                x = products[k][w] + local[group]
                total[group] = x
                square = square + x * x
        mean = jnp.sum(square, axis=2, keepdims=True)
        mean = jnp.broadcast_to(mean, (length, 8, lanes))
        shift = reqs
        while shift < 8:
            mean = mean + pltpu.roll(mean, shift, 1)
            shift *= 2
        scale = lax.rsqrt(mean * (1.0 / width) + 1e-05)

        def step(group, carry):
            gate = jax.nn.sigmoid(gates[:, group].astype(F32))
            out[:, group] = (total[group] * scale * gain[group][None] * gate).astype(BF16)
            return carry

        lax.fori_loop(0, groups, step, 0)

    return call(
        kernel, jax.ShapeDtypeStruct((length, groups, 8, lanes), BF16), [SMEM] + [VMEM] * (half + 3), VMEM,
        [pltpu.VMEM((groups, length, 8, lanes), F32)], (place, *products, local, gates, gain),
        flops=10 * local.size, moved=10 * local.size,
    )


def whole_heads(n, queries, key_vectors, values, gate_logits, decay_rates, norm_gain, pool_states, pool_entry):
    reqs, length, feature_width = queries.shape
    head_count = decay_rates.shape[0]
    lanes = pool_states.shape[2]
    heads = head_count // n
    half = n // 2

    def tiled(x):
        x = x.reshape(reqs, length, head_count, lanes).transpose(1, 2, 0, 3)
        return x.reshape(length, n, 8, lanes)

    def shift(x, k):
        return lax.ppermute(x, "batch", [(i, (i + k) % n) for i in range(n)])

    def shift_half(x, k):
        return lax.ppermute(x, "batch", [(i, i // half * half + (i + k) % half) for i in range(n)])

    q, k, v, gates = (tiled(x) for x in (queries, key_vectors, values, gate_logits))
    gain = jnp.repeat(norm_gain.reshape(n, heads, 1, lanes), reqs, axis=2).reshape(n, 8, lanes)
    place = lax.axis_index("batch").reshape(1)
    entries = lax.all_to_all(
        jnp.broadcast_to(pool_entry[None], (n, reqs)), "batch", 0, 0, tiled=True
    ).reshape(n * reqs)

    pool_out, query_out = pack_start(place, pool_states.reshape(n, heads * lanes, lanes), q, n)
    pools = [pool_out[0]] + [shift(pool_out[d % half], d) for d in range(1, n)]
    asked = [query_out[0]] + [shift_half(query_out[d], d) for d in range(1, half)]
    local = in_block(decay_rates, q, k, v, query_out[0], heads)
    pair_out = pack_pairs(place, k, v, (pools[n // 2],), n)
    pairs = [pair_out[0]] + [shift(pair_out[d], d) for d in range(1, n)]
    answers = from_state(place, entries, decay_rates, pools, asked, n, heads)
    products = [answers[0]] + [shift_half(answers[d], half - d) for d in range(1, half)]
    mixed = finish(place, products, local, gates, gain, n, heads)
    states = None
    for first in range(0, n, half):
        ks = range(first, first + half)
        states = next_states(
            place, entries, decay_rates, pools, [pairs[d] for d in ks], states, ks, n, heads
        )
    mixed = mixed.reshape(length, head_count, reqs, lanes).transpose(2, 0, 1, 3)
    return (mixed.reshape(reqs, length, feature_width), states)


def solution(mesh):
    n = mesh.shape["batch"]

    def on_device(*args):
        reqs = args[0].shape[0]
        head_count = args[4].shape[0]
        entries, _, lanes = args[6].shape
        heads = head_count // n
        if n % 2 == 0 and entries == 1 and lanes == 128 and heads * n == head_count and heads * reqs == 8:
            return whole_heads(n, *args)
        return general(*args)

    placed = (
        P(("groups", "batch"), None, None),
        P(("groups", "batch"), None, None),
        P(("groups", "batch"), None, None),
        P(("groups", "batch"), None, None),
        P(),
        P(),
        P(("groups", "batch"), None, None),
        P(("groups", "batch")),
    )
    return jax.shard_map(
        on_device,
        mesh=mesh,
        in_specs=placed,
        out_specs=(P(("groups", "batch"), None, None), P("groups", "batch", None)),
        check_vma=False,
    )
```

```python
import jax
import jax.numpy as jnp
from jax import lax
from jax.experimental import pallas as pl
from jax.experimental.pallas import tpu as pltpu
from jax.sharding import PartitionSpec as P


ANY = pl.BlockSpec(memory_space=pl.ANY)
SMEM = pl.BlockSpec(memory_space=pltpu.SMEM)
VMEM = pl.BlockSpec(memory_space=pltpu.VMEM)
F32 = jnp.float32
BF16 = jnp.bfloat16
NT = (((1,), (1,)), ((), ()))
TN = (((0,), (0,)), ((), ()))


def finish_output(attended, gate_logits, norm_gain):
    mean_square = jnp.mean(attended * attended, axis=-1, keepdims=True)
    scaled = attended * lax.rsqrt(mean_square + 1e-05) * norm_gain
    return (scaled * jax.nn.sigmoid(gate_logits.astype(jnp.float32))).astype(jnp.bfloat16)


def attend(query_part, key_part, value_part, resumed, rates_here):
    length = query_part.shape[1]
    highest = lax.Precision.HIGHEST
    positions = jnp.arange(1, length + 1).astype(jnp.float32)
    decay_now = jnp.exp(-positions[:, None] * rates_here[None, :])
    from_state = jnp.einsum(
        "rtgd,rgde->rtge", query_part, resumed, preferred_element_type=jnp.float32
    )
    from_state = from_state * decay_now[None, :, :, None]
    key_wide = key_part.astype(jnp.float32)
    value_wide = value_part.astype(jnp.float32)
    distance = positions[:, None] - positions[None, :]
    decay_pair = jnp.where(
        (distance >= 0.0)[:, :, None],
        jnp.exp(-jnp.maximum(distance, 0.0)[:, :, None] * rates_here),
        0.0,
    )
    scores = (
        jnp.einsum("rtgd,rsgd->rtsg", query_part, key_part, preferred_element_type=jnp.float32)
        * decay_pair[None]
    )
    in_block = jnp.einsum("rtsg,rsge->rtge", scores, value_wide, precision=highest)
    tail_decay = jnp.exp(-(float(length) - positions)[:, None] * rates_here[None, :])
    weighted_keys = key_wide * tail_decay[None, :, :, None]
    updated = jnp.exp(-float(length) * rates_here)[None, :, None, None] * resumed.astype(
        jnp.float32
    )
    updated = updated + jnp.einsum("rsgd,rsge->rgde", weighted_keys, value_wide, precision=highest)
    return (from_state + in_block, updated)


def general(
    queries, key_vectors, values, gate_logits, decay_rates, norm_gain, pool_states, pool_entry
):
    req_dev, length, feature_width = queries.shape
    head_count = decay_rates.shape[0]
    head_size = pool_states.shape[2]
    entries = lax.all_gather(pool_entry, "batch", axis=0, tiled=True)
    spread = lax.all_to_all(pool_states, "batch", split_axis=1, concat_axis=0, tiled=True)
    chosen = jnp.take(spread, entries, axis=0)
    resumed = lax.all_to_all(chosen, "batch", split_axis=0, concat_axis=1, tiled=True)
    resumed = resumed.reshape(req_dev, head_count, head_size, head_size)
    shaped = (req_dev, length, head_count, head_size)
    attended, updated = attend(
        queries.reshape(shaped),
        key_vectors.reshape(shaped),
        values.reshape(shaped),
        resumed,
        decay_rates,
    )
    attended = attended.reshape(req_dev, length, feature_width)
    local_states = updated.astype(jnp.bfloat16).reshape(req_dev, feature_width, head_size)
    new_states = lax.all_to_all(local_states, "batch", split_axis=1, concat_axis=0, tiled=True)
    mixed = finish_output(attended, gate_logits, norm_gain)
    return (mixed, new_states)


def call(kernel, outs, in_specs, out_specs, scratch, args, flops=0, moved=0, aliases=None):
    return pl.pallas_call(
        kernel,
        out_shape=outs,
        in_specs=in_specs,
        out_specs=out_specs,
        scratch_shapes=scratch,
        input_output_aliases=aliases or {},
        compiler_params=pltpu.CompilerParams(vmem_limit_bytes=48 * 1024 * 1024),
        cost_estimate=pl.CostEstimate(flops=flops, bytes_accessed=moved, transcendentals=0),
    )(*args)


def row_rates(rates, group, heads):
    head = lax.broadcasted_iota(jnp.int32, (8, 128), 0) // (8 // heads)
    rate = jnp.full((8, 128), rates[group * heads], F32)
    for h in range(1, heads):
        rate = jnp.where(head == h, rates[group * heads + h], rate)
    return rate


def pack_pool(place, mine, pool, n):
    half = n // 2
    _, rows, lanes = pool.shape
    reqs = mine.shape[0]

    def kernel(place, mine, pool, *refs):
        outs = refs[:half]
        buf, tile, load, store = refs[half:]
        spot = lax.rem(place[0], half)
        loads = [
            pltpu.make_async_copy(pool.at[pl.ds(w * half, half)], buf.at[pl.ds(w * half, half)], load.at[w])
            for w in range(2)
        ]
        for copy in loads:
            copy.start()
        lane = lax.broadcasted_iota(jnp.int32, (8, lanes), 1)
        number = jnp.zeros((8, lanes), jnp.int32)
        for i in range(reqs):
            number = jnp.where(lane == i, mine[i], number)
        tile[...] = number.astype(F32).astype(BF16)
        stores = [
            pltpu.make_async_copy(tile, outs[d].at[pl.ds(2 * rows, 8)], store.at[d, 2]) for d in range(half)
        ]
        for copy in stores:
            copy.start()
        for w in range(2):
            loads[w].wait()
            for d in range(half):
                there = (spot ^ d) + w * half
                stores.append(
                    pltpu.make_async_copy(buf.at[there], outs[d].at[pl.ds(w * rows, rows)], store.at[d, w])
                )
                stores[-1].start()
        for copy in stores:
            copy.wait()

    scratch = [
        pltpu.VMEM(pool.shape, BF16),
        pltpu.VMEM((8, lanes), BF16),
        pltpu.SemaphoreType.DMA((2,)),
        pltpu.SemaphoreType.DMA((half, 3)),
    ]
    return call(
        kernel, [jax.ShapeDtypeStruct((2 * rows + 8, lanes), BF16)] * half, [SMEM, SMEM, ANY], [ANY] * half,
        scratch, (place, mine, pool), moved=4 * pool.size,
    )


def pack_queries(place, queries, after, n):
    half = n // 2
    length, _, _, lanes = queries.shape

    def kernel(place, queries, after, *refs):
        outs = refs[:half]
        buf, load, store = refs[half:]
        spot = lax.rem(place[0], half)
        copy = pltpu.make_async_copy(queries, buf, load)
        copy.start()
        copy.wait()
        stores = []
        for w in range(2):
            for d in range(half):
                there = (spot ^ d) + w * half
                stores.append(pltpu.make_async_copy(buf.at[:, there], outs[d].at[w], store.at[d, w]))
                stores[-1].start()
        for copy in stores:
            copy.wait()

    scratch = [
        pltpu.VMEM(queries.shape, BF16),
        pltpu.SemaphoreType.DMA,
        pltpu.SemaphoreType.DMA((half, 2)),
    ]
    return call(
        kernel, [jax.ShapeDtypeStruct((2, length, 8, lanes), BF16)] * half, [SMEM, ANY, ANY], [ANY] * half,
        scratch, (place, queries, after), moved=4 * queries.size,
    )


def pack_pairs(place, keys, values, after, n):
    length, _, _, lanes = keys.shape

    def kernel(place, keys, values, *refs):
        outs = refs[len(after) : len(after) + n]
        buf, load, store = refs[len(after) + n :]
        me = place[0]
        loads = [
            pltpu.make_async_copy(source, buf.at[w], load.at[w]) for w, source in enumerate((keys, values))
        ]
        for copy in loads:
            copy.start()
        stores = []
        for w in range(2):
            loads[w].wait()
            for k in range(n):
                there = me ^ k
                stores.append(pltpu.make_async_copy(buf.at[w, :, there], outs[k].at[w], store.at[k, w]))
                stores[-1].start()
        for copy in stores:
            copy.wait()

    outs = [jax.ShapeDtypeStruct((2, length, 8, lanes), BF16)] * n
    scratch = [
        pltpu.VMEM((2,) + keys.shape, BF16),
        pltpu.SemaphoreType.DMA((2,)),
        pltpu.SemaphoreType.DMA((n, 2)),
    ]
    return call(
        kernel, outs, [SMEM] + [ANY] * (2 + len(after)), [ANY] * n, scratch, (place, keys, values, *after),
        moved=8 * keys.size,
    )


def in_block(rates, queries, keys, values, after, heads):
    length, groups, _, lanes = queries.shape
    rows = length * 8

    def kernel(rates, q_ref, k_ref, v_ref, after_ref, out_ref, gap):
        group = pl.program_id(0)

        @pl.when(group == 0)
        def _():
            row = lax.broadcasted_iota(jnp.int32, (rows, rows), 0)
            column = lax.broadcasted_iota(jnp.int32, (rows, rows), 1)
            distance = (row >> 3) - (column >> 3)
            seen = ((row & 7) == (column & 7)) & (distance >= 0)
            gap[...] = jnp.where(seen, distance, -1).astype(F32)

        def flat(ref):
            return ref[:, 0].astype(F32).reshape(rows, lanes).astype(BF16)

        q, k, v = flat(q_ref), flat(k_ref), flat(v_ref)
        rate = row_rates(rates, group, heads)[:, :1]
        rate = jnp.broadcast_to(rate[None], (length, 8, 1)).reshape(rows, 1)
        distance = gap[...]
        decay = jnp.where(distance >= 0.0, jnp.exp(-jnp.maximum(distance, 0.0) * rate), 0.0)
        scores = lax.dot_general(q, k, NT, preferred_element_type=F32) * decay
        coarse = scores.astype(BF16)
        fine = (scores - coarse.astype(F32)).astype(BF16)
        total = jnp.dot(coarse, v, preferred_element_type=F32)
        total = total + jnp.dot(fine, v, preferred_element_type=F32)
        out_ref[0] = total.reshape(length, 8, lanes)

    block = pl.BlockSpec((length, 1, 8, lanes), lambda g: (0, g, 0, 0))
    return pl.pallas_call(
        kernel,
        grid=(groups,),
        out_shape=jax.ShapeDtypeStruct((groups, length, 8, lanes), F32),
        in_specs=[SMEM, block, block, block, ANY],
        out_specs=pl.BlockSpec((1, length, 8, lanes), lambda g: (g, 0, 0, 0)),
        scratch_shapes=[pltpu.VMEM((rows, rows), F32)],
        compiler_params=pltpu.CompilerParams(vmem_limit_bytes=32 * 1024 * 1024),
        cost_estimate=pl.CostEstimate(
            flops=6 * groups * rows * rows * lanes, bytes_accessed=10 * queries.size, transcendentals=0
        ),
    )(rates, queries, keys, values, after)


def from_state(place, rates, pools, queries, after, n, heads):
    half = n // 2
    reqs = 8 // heads
    _, length, _, lanes = queries[0].shape
    width = heads * lanes
    rows = length * 8

    def kernel(place, rates, *refs):
        pool_in, query_in = refs[:n], refs[n : n + half]
        outs, table_out = refs[n + half + 1 : n + 2 * half + 1], refs[n + 2 * half + 1]
        pool_buf, query_buf, out_buf, listed, table, pool_sem, query_sem, out_sem, table_sem = refs[n + 2 * half + 2 :]
        me = place[0]
        spot = lax.rem(me, half)
        loads = [pltpu.make_async_copy(pool_in[d], pool_buf.at[d], pool_sem.at[d]) for d in range(n)]
        asked = [pltpu.make_async_copy(query_in[d], query_buf.at[d], query_sem.at[d]) for d in range(half)]
        for copy in loads + asked:
            copy.start()
        for copy in loads:
            copy.wait()
        for d in range(n):
            numbers = pool_buf[d, 2 * width : 2 * width + 8, :].astype(F32)
            listed[d : d + 1, :] = numbers[:1].astype(jnp.int32)
        copies = [
            pltpu.make_async_copy(listed, table, table_sem.at[0]),
            pltpu.make_async_copy(listed, table_out, table_sem.at[1]),
        ]
        for copy in copies:
            copy.start()
        for copy in copies + asked:
            copy.wait()
        row = lax.broadcasted_iota(jnp.int32, (length, 8, lanes), 1)
        time = (lax.broadcasted_iota(jnp.int32, (length, 8, lanes), 0) + 1).astype(F32)

        for w in range(2):
            decay = jnp.exp(-time * row_rates(rates, spot + w * half, heads)[None])

            def step(d, carry):
                slots = [me ^ table[d, i] for i in range(reqs)]
                q = query_buf[d, w].astype(F32)
                total = jnp.zeros((rows, lanes), F32)
                for h in range(heads):
                    parts, states = [], []
                    for i in range(reqs):
                        parts.append(jnp.where(row == h * reqs + i, q, 0.0).reshape(rows, lanes).astype(BF16))
                        states.append(pool_buf[slots[i], (w * heads + h) * lanes : (w * heads + h + 1) * lanes, :])
                    total = total + jnp.dot(
                        jnp.concatenate(parts, axis=1),
                        jnp.concatenate(states, axis=0),
                        preferred_element_type=F32,
                    )
                out_buf[d, w] = total.reshape(length, 8, lanes) * decay
                return carry

            lax.fori_loop(0, half, step, 0)
        stores = [pltpu.make_async_copy(out_buf.at[d], outs[d], out_sem.at[d]) for d in range(half)]
        for copy in stores:
            copy.start()
        for copy in stores:
            copy.wait()

    outs = [jax.ShapeDtypeStruct((2, length, 8, lanes), F32)] * half
    outs.append(jax.ShapeDtypeStruct((n, lanes), jnp.int32))
    scratch = [
        pltpu.VMEM((n, 2 * width + 8, lanes), BF16),
        pltpu.VMEM((half, 2, length, 8, lanes), BF16),
        pltpu.VMEM((half, 2, length, 8, lanes), F32),
        pltpu.VMEM((n, lanes), jnp.int32),
        pltpu.SMEM((n, lanes), jnp.int32),
        pltpu.SemaphoreType.DMA((n,)),
        pltpu.SemaphoreType.DMA((half,)),
        pltpu.SemaphoreType.DMA((half,)),
        pltpu.SemaphoreType.DMA((2,)),
    ]
    got = call(
        kernel, outs, [SMEM] * 2 + [ANY] * (n + half + 1), [ANY] * (half + 1), scratch,
        (place, rates, *pools, *queries, after),
        flops=4 * n * rows * lanes * 8 * lanes, moved=4 * n * width * lanes,
    )
    return got[:half], got[half]


def next_states(place, table, rates, pools, pairs, kept, first, n, heads):
    reqs = 8 // heads
    _, length, _, lanes = pairs[0].shape
    width = heads * lanes
    rows = length * 8
    count = len(pairs)
    half = n // 2
    extra = 0 if kept is None else 1

    def kernel(place, table, rates, *refs):
        pool_in, pair_in = refs[:n], refs[n : n + count]
        out = refs[n + count + extra]
        pool_buf, pair_buf, key_buf, value_buf, out_buf, pool_sem, pair_sem, out_sem = refs[n + count + extra + 1 :]
        me = place[0]
        own = pl.multiple_of((me // half) * width, width)
        loads = [pltpu.make_async_copy(pair_in[k], pair_buf.at[k], pair_sem.at[k]) for k in range(count)]
        loads += [
            pltpu.make_async_copy(pool_in[d].at[pl.ds(own, width)], pool_buf.at[d], pool_sem.at[d]) for d in range(n)
        ]
        for copy in loads:
            copy.start()
        for copy in loads:
            copy.wait()
        left = (length - 1 - lax.broadcasted_iota(jnp.int32, (length, 8, lanes), 0)).astype(F32)
        weight = jnp.exp(-left * row_rates(rates, me, heads)[None])

        def step(c, carry):
            d = first + c
            source = me ^ d
            key_buf[...] = (pair_buf[c, 0].astype(F32) * weight).reshape(rows, lanes)
            value_buf[...] = pair_buf[c, 1].astype(F32).reshape(rows, lanes)
            for i in range(reqs):
                slot = me ^ table[d, i]
                for h in range(heads):
                    r = h * reqs + i
                    key = key_buf[pl.ds(r, length, stride=8), :]
                    value = value_buf[pl.ds(r, length, stride=8), :].astype(BF16)
                    coarse = key.astype(BF16)
                    fine = (key - coarse.astype(F32)).astype(BF16)
                    both = lax.dot_general(
                        jnp.concatenate([coarse, fine], axis=1), value, TN, preferred_element_type=F32
                    )
                    shrink = jnp.exp(jnp.full((1, lanes), -float(length) * rates[me * heads + h], F32))
                    start = pool_buf[slot, h * lanes : (h + 1) * lanes, :].astype(F32)
                    state = shrink * start + (both[:lanes] + both[lanes:])
                    out_buf[c * reqs + i, h * lanes : (h + 1) * lanes, :] = state.astype(BF16)
                pltpu.make_async_copy(
                    out_buf.at[c * reqs + i], out.at[source * reqs + i], out_sem.at[c * reqs + i]
                ).start()
            return carry

        lax.fori_loop(0, count, step, 0)
        for c in range(count * reqs):
            pltpu.make_async_copy(out_buf.at[c], out.at[c], out_sem.at[c]).wait()

    scratch = [
        pltpu.VMEM((n, width, lanes), BF16),
        pltpu.VMEM((count, 2, length, 8, lanes), BF16),
        pltpu.VMEM((rows, lanes), F32),
        pltpu.VMEM((rows, lanes), F32),
        pltpu.VMEM((count * reqs, width, lanes), BF16),
        pltpu.SemaphoreType.DMA((n,)),
        pltpu.SemaphoreType.DMA((count,)),
        pltpu.SemaphoreType.DMA((count * reqs,)),
    ]
    args = (place, table, rates, *pools, *pairs)
    aliases = None
    if kept is not None:
        aliases = {len(args): 0}
        args += (kept,)
    return call(
        kernel, jax.ShapeDtypeStruct((n * reqs, width, lanes), BF16),
        [SMEM] * 3 + [ANY] * (len(args) - 3), ANY, scratch, args,
        flops=count * 8 * 4 * lanes * lanes * length, moved=2 * n * width * lanes + 4 * count * width * lanes,
        aliases=aliases,
    )


def finish(place, products, local, gates, gain, n, heads):
    half = n // 2
    groups, length, _, lanes = local.shape
    reqs = 8 // heads
    width = groups * heads * lanes

    def kernel(place, *refs):
        products, local, gates, gain, out, total = refs[:half], *refs[half:]
        spot = lax.rem(place[0], half)
        square = jnp.zeros((length, 8, lanes), F32)
        for k in range(half):
            for w in range(2):
                group = (spot ^ k) + w * half
                x = products[k][w] + local[group]
                total[group] = x
                square = square + x * x
        mean = jnp.sum(square, axis=2, keepdims=True)
        mean = jnp.broadcast_to(mean, (length, 8, lanes))
        shift = reqs
        while shift < 8:
            mean = mean + pltpu.roll(mean, shift, 1)
            shift *= 2
        scale = lax.rsqrt(mean * (1.0 / width) + 1e-05)

        def step(group, carry):
            gate = jax.nn.sigmoid(gates[:, group].astype(F32))
            out[:, group] = (total[group] * scale * gain[group][None] * gate).astype(BF16)
            return carry

        lax.fori_loop(0, groups, step, 0)

    return call(
        kernel, jax.ShapeDtypeStruct((length, groups, 8, lanes), BF16), [SMEM] + [VMEM] * (half + 3), VMEM,
        [pltpu.VMEM((groups, length, 8, lanes), F32)], (place, *products, local, gates, gain),
        flops=10 * local.size, moved=10 * local.size,
    )


def PAIR_AFTER():
    return ()


def SPLIT(n):
    return ((0, n // 2), (n // 2, n))


def whole_heads(n, queries, key_vectors, values, gate_logits, decay_rates, norm_gain, pool_states, pool_entry):
    reqs, length, feature_width = queries.shape
    head_count = decay_rates.shape[0]
    lanes = pool_states.shape[2]
    heads = head_count // n
    half = n // 2

    def tiled(x):
        x = x.reshape(reqs, length, head_count, lanes).transpose(1, 2, 0, 3)
        return x.reshape(length, n, 8, lanes)

    def swap(x, d):
        return lax.ppermute(x, "batch", [(i, i ^ d) for i in range(n)])

    near, far = range(1, half), range(half, n)
    q, k, v, gates = (tiled(x) for x in (queries, key_vectors, values, gate_logits))
    gain = jnp.repeat(norm_gain.reshape(n, heads, 1, lanes), reqs, axis=2).reshape(n, 8, lanes)
    place = lax.axis_index("batch").reshape(1)

    pool_out = pack_pool(place, pool_entry, pool_states.reshape(n, heads * lanes, lanes), n)
    pools = {d: swap(pool_out[d % half], d) for d in (*far, *near)}
    pools = [pool_out[0]] + [pools[d] for d in range(1, n)]
    query_out = pack_queries(place, q, pool_out[0], n)
    asked = [query_out[0]] + [swap(query_out[d], d) for d in near]
    local = in_block(decay_rates, q, k, v, query_out[0], heads)
    pair_out = pack_pairs(place, k, v, (local,) + PAIR_AFTER(), n)
    pairs = {d: swap(pair_out[d], d) for d in (*far, *near)}
    pairs = [pair_out[0]] + [pairs[d] for d in range(1, n)]
    answers, table = from_state(place, decay_rates, pools, asked, pair_out[0], n, heads)
    products = [answers[0]] + [swap(answers[d], d) for d in near]
    states = None
    for first, last in SPLIT(n):
        states = next_states(place, table, decay_rates, pools, pairs[first:last], states, first, n, heads)
    mixed = finish(place, products, local, gates, gain, n, heads)
    mixed = mixed.reshape(length, head_count, reqs, lanes).transpose(2, 0, 1, 3)
    return (mixed.reshape(reqs, length, feature_width), states)


def solution(mesh):
    n = mesh.shape["batch"]

    def on_device(*args):
        reqs = args[0].shape[0]
        head_count = args[4].shape[0]
        entries, _, lanes = args[6].shape
        heads = head_count // n
        if n > 1 and n & (n - 1) == 0 and entries == 1 and lanes == 128 and heads * n == head_count and heads * reqs == 8:
            return whole_heads(n, *args)
        return general(*args)

    placed = (
        P(("groups", "batch"), None, None),
        P(("groups", "batch"), None, None),
        P(("groups", "batch"), None, None),
        P(("groups", "batch"), None, None),
        P(),
        P(),
        P(("groups", "batch"), None, None),
        P(("groups", "batch")),
    )
    return jax.shard_map(
        on_device,
        mesh=mesh,
        in_specs=placed,
        out_specs=(P(("groups", "batch"), None, None), P("groups", "batch", None)),
        check_vma=False,
    )
```

```python
import jax
import jax.numpy as jnp
from jax import lax
from jax.experimental import pallas as pl
from jax.experimental.pallas import tpu as pltpu
from jax.sharding import PartitionSpec as P


ANY = pl.BlockSpec(memory_space=pl.ANY)
HBM = pl.BlockSpec(memory_space=pltpu.HBM)
SMEM = pl.BlockSpec(memory_space=pltpu.SMEM)
VMEM = pl.BlockSpec(memory_space=pltpu.VMEM)
F32 = jnp.float32
BF16 = jnp.bfloat16
NT = (((1,), (1,)), ((), ()))
TN = (((0,), (0,)), ((), ()))


def finish_output(attended, gate_logits, norm_gain):
    mean_square = jnp.mean(attended * attended, axis=-1, keepdims=True)
    scaled = attended * lax.rsqrt(mean_square + 1e-05) * norm_gain
    return (scaled * jax.nn.sigmoid(gate_logits.astype(jnp.float32))).astype(jnp.bfloat16)


def attend(query_part, key_part, value_part, resumed, rates_here):
    length = query_part.shape[1]
    highest = lax.Precision.HIGHEST
    positions = jnp.arange(1, length + 1).astype(jnp.float32)
    decay_now = jnp.exp(-positions[:, None] * rates_here[None, :])
    from_state = jnp.einsum(
        "rtgd,rgde->rtge", query_part, resumed, preferred_element_type=jnp.float32
    )
    from_state = from_state * decay_now[None, :, :, None]
    key_wide = key_part.astype(jnp.float32)
    value_wide = value_part.astype(jnp.float32)
    distance = positions[:, None] - positions[None, :]
    decay_pair = jnp.where(
        (distance >= 0.0)[:, :, None],
        jnp.exp(-jnp.maximum(distance, 0.0)[:, :, None] * rates_here),
        0.0,
    )
    scores = (
        jnp.einsum("rtgd,rsgd->rtsg", query_part, key_part, preferred_element_type=jnp.float32)
        * decay_pair[None]
    )
    in_block = jnp.einsum("rtsg,rsge->rtge", scores, value_wide, precision=highest)
    tail_decay = jnp.exp(-(float(length) - positions)[:, None] * rates_here[None, :])
    weighted_keys = key_wide * tail_decay[None, :, :, None]
    updated = jnp.exp(-float(length) * rates_here)[None, :, None, None] * resumed.astype(
        jnp.float32
    )
    updated = updated + jnp.einsum("rsgd,rsge->rgde", weighted_keys, value_wide, precision=highest)
    return (from_state + in_block, updated)


def general(
    queries, key_vectors, values, gate_logits, decay_rates, norm_gain, pool_states, pool_entry
):
    req_dev, length, feature_width = queries.shape
    head_count = decay_rates.shape[0]
    head_size = pool_states.shape[2]
    entries = lax.all_gather(pool_entry, "batch", axis=0, tiled=True)
    spread = lax.all_to_all(pool_states, "batch", split_axis=1, concat_axis=0, tiled=True)
    chosen = jnp.take(spread, entries, axis=0)
    resumed = lax.all_to_all(chosen, "batch", split_axis=0, concat_axis=1, tiled=True)
    resumed = resumed.reshape(req_dev, head_count, head_size, head_size)
    shaped = (req_dev, length, head_count, head_size)
    attended, updated = attend(
        queries.reshape(shaped),
        key_vectors.reshape(shaped),
        values.reshape(shaped),
        resumed,
        decay_rates,
    )
    attended = attended.reshape(req_dev, length, feature_width)
    local_states = updated.astype(jnp.bfloat16).reshape(req_dev, feature_width, head_size)
    new_states = lax.all_to_all(local_states, "batch", split_axis=1, concat_axis=0, tiled=True)
    mixed = finish_output(attended, gate_logits, norm_gain)
    return (mixed, new_states)


def call(kernel, outs, in_specs, out_specs, scratch, args, flops=0, moved=0, aliases=None):
    return pl.pallas_call(
        kernel,
        out_shape=outs,
        in_specs=in_specs,
        out_specs=out_specs,
        scratch_shapes=scratch,
        input_output_aliases=aliases or {},
        compiler_params=pltpu.CompilerParams(vmem_limit_bytes=48 * 1024 * 1024),
        cost_estimate=pl.CostEstimate(flops=flops, bytes_accessed=moved, transcendentals=0),
    )(*args)


def row_rates(rates, group, heads):
    head = lax.broadcasted_iota(jnp.int32, (8, 128), 0) // (8 // heads)
    rate = jnp.full((8, 128), rates[group * heads], F32)
    for h in range(1, heads):
        rate = jnp.where(head == h, rates[group * heads + h], rate)
    return rate


def entry_tile(mine):
    lane = lax.broadcasted_iota(jnp.int32, (8, 128), 1)
    number = jnp.zeros((8, 128), jnp.int32)
    for i in range(mine.shape[0]):
        number = jnp.where(lane == i, mine[i], number)
    return number.astype(F32).astype(BF16)


def pack_far(place, mine, pool, n):
    half = n // 2
    _, rows, lanes = pool.shape

    def kernel(place, mine, pool, *outs):
        tile = entry_tile(mine)
        for c in range(half):
            outs[c][:rows, :] = pool[place[0] ^ (half + c)]
            outs[c][rows : 2 * rows, :] = pool[place[0] ^ c]
            outs[c][2 * rows :, :] = tile

    return call(
        kernel, [jax.ShapeDtypeStruct((2 * rows + 8, lanes), BF16)] * half, [SMEM, SMEM, VMEM], [VMEM] * half, [],
        (place, mine, pool), moved=4 * pool.size,
    )


def pack_near(place, mine, pool, queries, keys, values, after, n):
    half = n // 2
    _, tiles, _, lanes = pool.shape
    length = queries.shape[0]

    def kernel(place, mine, pool, queries, keys, values, after, *outs):
        me = place[0]
        tile = entry_tile(mine)
        for c in range(half):
            here, there = me ^ c, me ^ (c + half)
            at = 0
            for part in (pool[here], tile[None], queries[:, here], queries[:, there], pool[there], keys[:, here], values[:, here]):
                outs[c][at : at + part.shape[0]] = part
                at += part.shape[0]

    return call(
        kernel, [jax.ShapeDtypeStruct((2 * tiles + 1 + 4 * length, 8, lanes), BF16)] * half,
        [SMEM, SMEM] + [VMEM] * 4 + [ANY], [VMEM] * half, [], (place, mine, pool, queries, keys, values, after),
        moved=4 * pool.size + 8 * queries.size,
    )


def pack_pairs(place, keys, values, after, n):
    half = n // 2
    length, _, _, lanes = keys.shape

    def kernel(place, keys, values, after, *outs):
        for c in range(half):
            for w, source in enumerate((keys, values)):
                outs[c][w * length : (w + 1) * length] = source[:, place[0] ^ (c + half)]

    return call(
        kernel, [jax.ShapeDtypeStruct((2 * length, 8, lanes), BF16)] * half, [SMEM, VMEM, VMEM, ANY], [VMEM] * half, [],
        (place, keys, values, after), moved=4 * keys.size,
    )


def in_block(rates, queries, keys, values, after, heads):
    length, groups, _, lanes = queries.shape
    rows = length * 8

    def kernel(rates, q_ref, k_ref, v_ref, after_ref, out_ref, gap):
        group = pl.program_id(0)

        @pl.when(group == 0)
        def _():
            row = lax.broadcasted_iota(jnp.int32, (rows, rows), 0)
            column = lax.broadcasted_iota(jnp.int32, (rows, rows), 1)
            distance = (row >> 3) - (column >> 3)
            seen = ((row & 7) == (column & 7)) & (distance >= 0)
            gap[...] = jnp.where(seen, distance, -1).astype(F32)

        def flat(ref):
            return ref[:, 0].astype(F32).reshape(rows, lanes).astype(BF16)

        q, k, v = flat(q_ref), flat(k_ref), flat(v_ref)
        rate = row_rates(rates, group, heads)[:, :1]
        rate = jnp.broadcast_to(rate[None], (length, 8, 1)).reshape(rows, 1)
        distance = gap[...]
        decay = jnp.where(distance >= 0.0, jnp.exp(-jnp.maximum(distance, 0.0) * rate), 0.0)
        scores = lax.dot_general(q, k, NT, preferred_element_type=F32) * decay
        coarse = scores.astype(BF16)
        fine = (scores - coarse.astype(F32)).astype(BF16)
        total = jnp.dot(coarse, v, preferred_element_type=F32)
        total = total + jnp.dot(fine, v, preferred_element_type=F32)
        out_ref[0] = total.reshape(length, 8, lanes)

    block = pl.BlockSpec((length, 1, 8, lanes), lambda g: (0, g, 0, 0))
    return pl.pallas_call(
        kernel,
        grid=(groups,),
        out_shape=jax.ShapeDtypeStruct((groups, length, 8, lanes), F32),
        in_specs=[SMEM, block, block, block, ANY],
        out_specs=pl.BlockSpec((1, length, 8, lanes), lambda g: (g, 0, 0, 0)),
        scratch_shapes=[pltpu.VMEM((rows, rows), F32)],
        compiler_params=pltpu.CompilerParams(vmem_limit_bytes=32 * 1024 * 1024),
        cost_estimate=pl.CostEstimate(
            flops=6 * groups * rows * rows * lanes, bytes_accessed=10 * queries.size, transcendentals=0
        ),
    )(rates, queries, keys, values, after)


def from_state(place, rates, near, far, after, n, heads, rows):
    half = n // 2
    reqs = 8 // heads
    lanes = near[0].shape[1]
    width = heads * lanes

    def kernel(place, rates, *refs):
        near_in, far_in, outs, table_out = refs[:half], refs[half:n], refs[n + 1 : n + half + 1], refs[n + half + 1]
        pool_buf, listed, table, table_sem = refs[n + half + 2 :]
        me = place[0]
        for d in range(n):
            tile = near_in[d][width : width + 8, :] if d < half else far_in[d - half][2 * width :, :]
            listed[d : d + 1, :] = tile.astype(F32)[:1].astype(jnp.int32)
        copy = pltpu.make_async_copy(listed, table, table_sem)
        copy.start()
        table_out[...] = listed[...]
        for w in range(2):
            held = w * (width + 8 + 2 * rows)
            for d in range(half):
                pool_buf[w, d] = near_in[d][held : held + width, :]
                pool_buf[w, half + d] = far_in[d][w * width : (w + 1) * width, :]
        index = lax.broadcasted_iota(jnp.int32, (rows, lanes), 0)
        row = index & 7
        time = ((index >> 3) + 1).astype(F32)
        copy.wait()
        for w in range(2):
            rate = jnp.broadcast_to(row_rates(rates, me ^ (half * w), heads)[None], (rows // 8, 8, lanes))
            decay = jnp.exp(-time * rate.reshape(rows, lanes))
            for d in range(half):
                slots = [me ^ table[d, i] for i in range(reqs)]
                skip = width + 8 + w * rows
                q = near_in[d][skip : skip + rows, :].astype(F32)
                total = jnp.zeros((rows, lanes), F32)
                for h in range(heads):
                    parts, states = [], []
                    for i in range(reqs):
                        parts.append(jnp.where(row == h * reqs + i, q, 0.0).astype(BF16))
                        states.append(pool_buf[w, slots[i], h * lanes : (h + 1) * lanes, :])
                    total = total + jnp.dot(
                        jnp.concatenate(parts, axis=1),
                        jnp.concatenate(states, axis=0),
                        preferred_element_type=F32,
                    )
                outs[d][w * rows : (w + 1) * rows, :] = total * decay

    outs = [jax.ShapeDtypeStruct((2 * rows, lanes), F32)] * half
    outs.append(jax.ShapeDtypeStruct((n, lanes), jnp.int32))
    scratch = [
        pltpu.VMEM((2, n, width, lanes), BF16),
        pltpu.VMEM((n, lanes), jnp.int32),
        pltpu.SMEM((n, lanes), jnp.int32),
        pltpu.SemaphoreType.DMA,
    ]
    got = call(
        kernel, outs, [SMEM, SMEM] + [VMEM] * n + [ANY], [VMEM] * len(outs), scratch,
        (place, rates, *near, *far, after),
        flops=4 * n * rows * lanes * 8 * lanes, moved=4 * n * width * lanes,
    )
    return got[:half], got[half]


def next_states(place, table, rates, near, far, pairs, skip, kept, first, n, heads, rows):
    reqs = 8 // heads
    lanes = near[0].shape[1]
    width = heads * lanes
    length = rows // 8
    half = n // 2
    count = len(pairs)
    shared = pairs is near
    extra = 0 if kept is None else 1

    def kernel(place, table, rates, *refs):
        near_in, far_in = refs[:half], refs[half:n]
        pair_in = near_in if shared else refs[n : n + count]
        out, pool_buf, key_buf, value_buf, out_buf, out_sem = refs[n + (0 if shared else count) + extra :]
        me = place[0]
        for d in range(n):
            pool_buf[d] = (near_in[d] if d < half else far_in[d - half])[:width, :]
        index = lax.broadcasted_iota(jnp.int32, (rows, lanes), 0)
        left = (length - 1 - (index >> 3)).astype(F32)
        rate = jnp.broadcast_to(row_rates(rates, me, heads)[None], (length, 8, lanes))
        weight = jnp.exp(-left * rate.reshape(rows, lanes))
        copies = []
        for c in range(count):
            d = first + c
            source = me ^ d
            part = c % 2
            key_buf[part] = pair_in[c][skip : skip + rows, :].astype(F32) * weight
            value_buf[part] = pair_in[c][skip + rows : skip + 2 * rows, :].astype(F32)
            for i in range(reqs):
                slot = me ^ table[d, i]
                for h in range(heads):
                    r = h * reqs + i
                    key = key_buf[part, pl.ds(r, length, stride=8), :]
                    value = value_buf[part, pl.ds(r, length, stride=8), :].astype(BF16)
                    coarse = key.astype(BF16)
                    fine = (key - coarse.astype(F32)).astype(BF16)
                    both = lax.dot_general(
                        jnp.concatenate([coarse, fine], axis=1), value, TN, preferred_element_type=F32
                    )
                    shrink = jnp.exp(jnp.full((1, lanes), -float(length) * rates[me * heads + h], F32))
                    start = pool_buf[slot, h * lanes : (h + 1) * lanes, :].astype(F32)
                    state = shrink * start + (both[:lanes] + both[lanes:])
                    out_buf[c * reqs + i, h * lanes : (h + 1) * lanes, :] = state.astype(BF16)
                copies.append(
                    pltpu.make_async_copy(
                        out_buf.at[c * reqs + i], out.at[source * reqs + i], out_sem.at[c * reqs + i]
                    )
                )
                copies[-1].start()
        for copy in copies:
            copy.wait()

    scratch = [
        pltpu.VMEM((n, width, lanes), BF16),
        pltpu.VMEM((2, rows, lanes), F32),
        pltpu.VMEM((2, rows, lanes), F32),
        pltpu.VMEM((count * reqs, width, lanes), BF16),
        pltpu.SemaphoreType.DMA((count * reqs,)),
    ]
    args = (place, table, rates, *near, *far, *(() if shared else pairs))
    specs = [SMEM] * 3 + [VMEM] * (len(args) - 3)
    aliases = None
    if kept is not None:
        aliases = {len(args): 0}
        args += (kept,)
        specs.append(ANY)
    return call(
        kernel, jax.ShapeDtypeStruct((n * reqs, width, lanes), BF16), specs, ANY, scratch, args,
        flops=count * 8 * 4 * lanes * lanes * length, moved=2 * n * width * lanes + 4 * count * width * lanes,
        aliases=aliases,
    )


def finish(place, products, local, gates, gain, n, heads):
    groups, length, _, lanes = local.shape
    reqs = 8 // heads
    width = groups * heads * lanes
    half = n // 2
    rows = length * 8

    def kernel(place, *refs):
        products, local, gates, gain, out, total = refs[:half], *refs[half:]
        me = place[0]
        square = jnp.zeros((length, 8, lanes), F32)
        for d in range(n):
            group = me ^ d
            w = d // half
            x = products[d % half][w * rows : (w + 1) * rows, :].reshape(length, 8, lanes) + local[group]
            total[group] = x
            square = square + x * x
        mean = jnp.sum(square, axis=2, keepdims=True)
        mean = jnp.broadcast_to(mean, (length, 8, lanes))
        shift = reqs
        while shift < 8:
            mean = mean + pltpu.roll(mean, shift, 1)
            shift *= 2
        scale = lax.rsqrt(mean * (1.0 / width) + 1e-05)

        def step(group, carry):
            gate = jax.nn.sigmoid(gates[:, group].astype(F32))
            out[:, group] = (total[group] * scale * gain[group][None] * gate).astype(BF16)
            return carry

        lax.fori_loop(0, groups, step, 0)

    return call(
        kernel, jax.ShapeDtypeStruct((length, groups, 8, lanes), BF16), [SMEM] + [VMEM] * (half + 3), VMEM,
        [pltpu.VMEM((groups, length, 8, lanes), F32)], (place, *products, local, gates, gain),
        flops=10 * local.size, moved=10 * local.size,
    )


def whole_heads(n, queries, key_vectors, values, gate_logits, decay_rates, norm_gain, pool_states, pool_entry):
    reqs, length, feature_width = queries.shape
    head_count = decay_rates.shape[0]
    lanes = pool_states.shape[2]
    heads = head_count // n
    half = n // 2

    def tiled(x):
        x = x.reshape(reqs, length, head_count, lanes).transpose(1, 2, 0, 3)
        return x.reshape(length, n, 8, lanes)

    def swap(x, d):
        return lax.ppermute(x, "batch", [(i, i ^ d) for i in range(n)])

    q, k, v, gates = (tiled(x) for x in (queries, key_vectors, values, gate_logits))
    gain = jnp.repeat(norm_gain.reshape(n, heads, 1, lanes), reqs, axis=2).reshape(n, 8, lanes)
    place = lax.axis_index("batch").reshape(1)
    width = heads * lanes
    rows = length * 8
    pool = pool_states.reshape(n, width, lanes)
    pool_tiles = pool_states.reshape(n, width // 8, 8, lanes)

    def flat(x):
        return x.reshape(-1, lanes)

    far_out = pack_far(place, pool_entry, pool, n)
    far = [swap(far_out[c], half + c) for c in range(half)]
    near_out = pack_near(place, pool_entry, pool_tiles, q, k, v, far_out[0], n)
    near = [flat(near_out[0])] + [flat(swap(near_out[c], c)) for c in range(1, half)]
    pair_out = pack_pairs(place, k, v, near_out[0], n)
    pairs = [flat(swap(pair_out[c], half + c)) for c in range(half)]
    local = in_block(decay_rates, q, k, v, near_out[0], heads)
    answers, table = from_state(place, decay_rates, near, far, pair_out[0], n, heads, rows)
    answers = [answers[0]] + [swap(answers[c], c) for c in range(1, half)]
    keep = 2 * width + 8 + 2 * rows
    states = next_states(place, table, decay_rates, near, far, near, keep, None, 0, n, heads, rows)
    states = next_states(place, table, decay_rates, near, far, pairs, 0, states, half, n, heads, rows)
    mixed = finish(place, answers, local, gates, gain, n, heads)
    mixed = mixed.reshape(length, head_count, reqs, lanes).transpose(2, 0, 1, 3)
    return (mixed.reshape(reqs, length, feature_width), states)


def solution(mesh):
    n = mesh.shape["batch"]

    def on_device(*args):
        reqs = args[0].shape[0]
        head_count = args[4].shape[0]
        entries, _, lanes = args[6].shape
        heads = head_count // n
        if n > 1 and n & (n - 1) == 0 and entries == 1 and lanes == 128 and heads * n == head_count and heads * reqs == 8:
            return whole_heads(n, *args)
        return general(*args)

    placed = (
        P(("groups", "batch"), None, None),
        P(("groups", "batch"), None, None),
        P(("groups", "batch"), None, None),
        P(("groups", "batch"), None, None),
        P(),
        P(),
        P(("groups", "batch"), None, None),
        P(("groups", "batch")),
    )
    return jax.shard_map(
        on_device,
        mesh=mesh,
        in_specs=placed,
        out_specs=(P(("groups", "batch"), None, None), P("groups", "batch", None)),
        check_vma=False,
    )
```
